128 devices in a mesh: term: 16 (over y, x_hi, core), sector: 8 (over x_lo, z).
Axes of the slice: x: 4 (x_hi: 2, x_lo: 2; x = x_hi * 2 + x_lo), y: 4, z: 4, core: 2. Of those that a mesh axis runs over, the one named last changes fastest.
Arguments:
- psi: float32 [16, 384, 4, 384], P('sector'), may hold values from -6 to 6
- precond: bfloat16 [16, 384, 4, 384], P('sector'), may hold values from 1 to 10
- left_environment_block: float32 [32, 16, 384, 384], P('term', 'sector'), may hold values from -0.3125 to 0.3125
- right_env: float32 [32, 16, 384, 384], P('term', 'sector'), may hold values from -0.3125 to 0.3125
- term_operators: float32 [32, 4, 4], P('term'), may hold values from -3 to 3
- term_charge: int32 [32], P('term'), may hold values from -1 to 1, as said below
- sector_sizes: int32 [16], P('sector'), may hold values from 128 to 384, as said below
- sector_energy: float32 [16], P('sector'), may hold values from 2 to 20
Outputs:
- psi_next: float32 [16, 384, 4, 384], P('sector', 'term')
- energies: float32 [1], replicated
The draws below stay inside these ranges and needn't reach their ends.
Inputs may be any that keep to these rules, and one draw needn't show every extreme that they name: `term_charge`: every value -1, 0 and 1 occurs. `sector_sizes`: some sector has exactly 384 states and some exactly 128.
All inputs are finite; a program needn't handle non-finite values.
Results may differ from the reference program's by a relative error of at most 0.0003.
Values sent between devices are 32-bit elements; how exact they have to be, the bound alone decides.
A program may use at most 128 MiB of HBM per device.

```python
import math
import jax
import jax.numpy as jnp
from jax import lax

MS = 384
P_SIZE = 4
UPDATES = 1
TERMS = 32
SECTORS = 16


def draw_term_charge(key, part):
    charge = jax.random.randint(key, (TERMS,), -1, 2).astype(jnp.int32)
    picks = jax.random.permutation(jax.random.fold_in(key, 7), TERMS)
    charge = charge.at[picks[0]].set(-1)
    charge = charge.at[picks[1]].set(1)
    charge = charge.at[picks[2]].set(0)
    return charge.astype(jnp.int32)


def draw_sector_sizes(key, part):
    sizes = jax.random.randint(key, (SECTORS,), MS // 3, MS + 1).astype(jnp.int32)
    picks = jax.random.permutation(jax.random.fold_in(key, 11), SECTORS)
    sizes = sizes.at[picks[0]].set(MS)
    sizes = sizes.at[picks[1]].set(MS // 3)
    return sizes.astype(jnp.int32)


def shard_levels(own_key, shape, cuts, least, largest):
    def one(dim, parts):
        draws = jax.random.uniform(jax.random.fold_in(jax.random.fold_in(own_key, 6), dim), (parts,), jnp.float32, least / len(cuts), largest / len(cuts))
        return jnp.repeat(jnp.exp(draws), shape[dim] // parts).reshape((-1,) + (1,) * (len(shape) - dim - 1))

    gain = one(*cuts[0])
    for cut in cuts[1:]:
        gain = gain * one(*cut)
    return gain


def normal_values(stream_key, dims, scale, bound, shards=(), kind=jnp.bfloat16):
    entries = scale * jax.random.normal(stream_key, dims, jnp.float32)
    if shards:
        entries = entries * shard_levels(stream_key, dims, shards, -0.22, 0.18)
    return jnp.clip(entries, -bound, bound).astype(kind)


def setup_inputs(seed: int = 0) -> dict:
    key_list = jax.random.split(jax.random.key(seed), 9)
    return {
        "psi": normal_values(key_list[0], (SECTORS, MS, P_SIZE, MS), 1.0, 6.0, ((0, 8),), jnp.float32),
        "precond": jnp.clip(jnp.exp(math.log(10.0) - 2.3025851 * jax.random.uniform(key_list[1], (SECTORS, MS, P_SIZE, MS), jnp.float32) ** shard_levels(key_list[1], (SECTORS, MS, P_SIZE, MS), ((0, 8),), -0.2, 0.2)), 1.0, 10.0).astype(jnp.bfloat16),
        "left_environment_block": normal_values(key_list[2], (TERMS, SECTORS, MS, MS), MS ** -0.5, 0.3125, ((0, 16), (1, 8)), jnp.float32),
        "right_env": normal_values(key_list[3], (TERMS, SECTORS, MS, MS), MS ** -0.5, 0.3125, ((0, 16), (1, 8)), jnp.float32),
        "term_operators": normal_values(key_list[4], (TERMS, P_SIZE, P_SIZE), P_SIZE ** -0.5, 3.0, ((0, 16),), jnp.float32),
        "term_charge": draw_term_charge(jax.random.fold_in(key_list[8], 71), 0),
        "sector_sizes": draw_sector_sizes(jax.random.fold_in(key_list[8], 71), 0),
        "sector_energy": jnp.clip(jnp.exp(math.log(20.0) - 2.3025851 * jax.random.uniform(key_list[7], (SECTORS,), jnp.float32) ** shard_levels(key_list[7], (SECTORS,), ((0, 8),), -0.2, 0.2)), 2.0, 20.0),
    }


EPSILON = 1e-06
TOP_LEVEL = lax.Precision.HIGHEST

def hamiltonian(state, left_environment_block, right_env, term_operators, term_charge, sector_energy, valid_mask):
    zero_block = jnp.zeros_like(state[:1])
    from_below = jnp.concatenate([zero_block, state[:-1]], axis=0)
    from_above = jnp.concatenate([state[1:], zero_block], axis=0)

    def single_term(total, inputs):
        left_side, right, operator, charge = inputs
        source_sector = jnp.where(charge == 1, from_below, jnp.where(charge == -1, from_above, state))
        leading_item = jnp.einsum('qom,qmsg->qosg', left_side, source_sector, precision=TOP_LEVEL)
        second = jnp.einsum('pr,tarb->tapb', operator, leading_item, precision=TOP_LEVEL)
        third = jnp.einsum('tape,teb->tapb', second, right, precision=TOP_LEVEL)
        return (total + third, None)
    total, _ = lax.scan(single_term, jnp.zeros_like(state), (left_environment_block, right_env, term_operators, term_charge))
    return (total + sector_energy[:, None, None, None] * state) * valid_mask

def reference(psi, precond, left_environment_block, right_env, term_operators, term_charge, sector_sizes, sector_energy):
    positions = jnp.arange(MS, dtype=jnp.int32)
    inside = positions[None, :] < sector_sizes[:, None]
    valid_mask = (inside[:, :, None, None] & inside[:, None, None, :]).astype(jnp.float32)
    precond_wide = precond.astype(jnp.float32)
    state = psi * valid_mask
    energies = []
    for update_step in range(UPDATES):
        image = hamiltonian(state, left_environment_block, right_env, term_operators, term_charge, sector_energy, valid_mask)
        energy = jnp.sum(state * image) / jnp.sum(state * state)
        moved = state - (image - energy * state) / precond_wide
        state = moved * lax.rsqrt(jnp.mean(moved * moved) + EPSILON)
        energies.append(energy)
    return (state, jnp.stack(energies))
```

```python
import functools

import jax
import jax.numpy as jnp
from jax import lax
from jax.experimental import pallas as pl
from jax.experimental.pallas import tpu as pltpu
from jax.sharding import PartitionSpec as P

EPSILON = 1e-06
F32 = jnp.float32
BF16 = jnp.bfloat16
MS = 384
PH = 4
LT = 3
CH = 128
NCH = MS // CH
OWN = MS // 16
WIDE = PH * MS
UNIT = WIDE // 2


def split(x):
    hi = x.astype(BF16)
    return hi, (x - hi.astype(F32)).astype(BF16)


def kernel(
    psi, precond, lenv, renv, ops, charge, sizes, energy,
    out, eng,
    ext0, ext1, ext2, extsz, szt, lbuf, rbuf, l3, r3, lhs, zbuf, rhs, acc,
    prx, cs, vrx, yrx, ysb, xrx, stb, pcb, stw, inv, img, ga, gb, gt,
    sem_in, sem_own, sem_lr, sem_hz, sem_hp, sem_sz, sem_p, sem_v, sem_y, sem_x, sem_ga, sem_gb,
):
    ext = (ext0, ext1, ext2)
    term = lax.axis_index("term")
    sec = lax.axis_index("sector")
    y = lax.div(term, 4)
    xh = lax.rem(lax.div(term, 2), 2)
    core = lax.rem(term, 2)

    def dev(yy, hh, cc, ss=None):
        return {"term": yy * 4 + hh * 2 + cc, "sector": sec if ss is None else ss}

    partner = dev(y, xh, 1 - core)
    yup, ydn, yop = lax.rem(y + 1, 4), lax.rem(y + 3, 4), lax.rem(y + 2, 4)
    up, down = dev(yup, xh, core), dev(ydn, xh, core)
    xpart = dev(y, 1 - xh, core)
    has_low, has_high = sec > 0, sec < 7
    above, below = dev(y, xh, core, sec + 1), dev(y, xh, core, sec - 1)

    me_a = y * 2 + core
    me_b = xh * 8 + sec

    def peer_a(i):
        return dev(lax.div(i, 2), xh, lax.rem(i, 2))

    def peer_b(i):
        return dev(y, lax.div(i, 8), core, lax.rem(i, 8))

    def rows_of(ref, first, n):
        return ref.at[pl.ds(pl.multiple_of(first * PH, 8), n * PH), :].reshape(n, PH, 128)

    loads = []
    for k in range(NCH):
        for s in range(2):
            for e in range(LT):
                loads.append(pltpu.make_async_copy(
                    psi.at[s, pl.ds(k * CH, CH), :, pl.ds(e * 128, 128)],
                    rows_of(ext[k].at[1 + s, e], 0, CH), sem_in.at[k, s, e]))
    own = [
        pltpu.make_async_copy(psi.at[:, pl.ds(term * OWN, OWN)], stb, sem_own.at[0]),
        pltpu.make_async_copy(precond.at[:, pl.ds(term * OWN, OWN)], pcb, sem_own.at[1]),
    ]
    cl = pltpu.make_async_copy(lenv, lbuf, sem_lr.at[0])
    cr = pltpu.make_async_copy(renv, rbuf, sem_lr.at[1])

    for s in range(2):
        szt[s] = jnp.full((8, 128), sizes[s], jnp.int32)
        extsz[1 + s] = jnp.full((8, 128), sizes[s], jnp.int32)

    barrier = pltpu.get_barrier_semaphore()
    for o in range(1, 8):
        pl.semaphore_signal(barrier, inc=1, device_id=peer_a(lax.rem(me_a + o, 8)), device_id_type=pl.DeviceIdType.MESH)
    for o in range(1, 16):
        pl.semaphore_signal(barrier, inc=1, device_id=peer_b(lax.rem(me_b + o, 16)), device_id_type=pl.DeviceIdType.MESH)
    cr.start()
    cl.start()
    for c in loads + own:
        c.start()
    pl.semaphore_wait(barrier, 22)

    def remote(src, dst, s, r, where):
        return pltpu.make_async_remote_copy(
            src_ref=src, dst_ref=dst, send_sem=s, recv_sem=r, device_id=where, device_id_type=pl.DeviceIdType.MESH)

    HALF = CH // 2
    hoff = core * HALF

    def halo(k, d, e):
        s, slot, where = ((1, 0, above), (0, 3, below))[d]
        return remote(
            psi.at[s, pl.ds(k * CH + hoff, HALF), :, pl.ds(e * 128, 128)],
            rows_of(ext[k].at[slot, e], hoff, HALF),
            sem_hz.at[0, k, d, e], sem_hz.at[1, k, d, e], where)

    def pass_on(k, d):
        ref = ext[k].at[(0, 3)[d], :, pl.ds(pl.multiple_of(hoff * PH, 8), HALF * PH), :]
        return remote(ref, ref, sem_hp.at[0, k, d], sem_hp.at[1, k, d], partner)

    def size_copy(d):
        s, slot, where = ((1, 0, above), (0, 3, below))[d]
        return remote(szt.at[s], extsz.at[slot], sem_sz.at[0, d], sem_sz.at[1, d], where)

    can_send = (has_high, has_low)
    can_get = (has_low, has_high)
    for d in range(2):
        @pl.when(can_send[d])
        def _():
            size_copy(d).start()
            for k in range(NCH):
                for e in range(LT):
                    halo(k, d, e).start()

        @pl.when(jnp.logical_not(can_get[d]))
        def _():
            extsz[(0, 3)[d]] = jnp.zeros((8, 128), jnp.int32)
            for k in range(NCH):
                ext[k][(0, 3)[d]] = jnp.zeros((LT, CH * PH, 128), F32)

    for d in range(2):
        @pl.when(can_get[d])
        def _():
            size_copy(d).wait_recv()

        @pl.when(can_send[d])
        def _():
            size_copy(d).wait_send()

    cr.wait()
    cl.wait()
    for w in range(2):
        for t in range(2):
            sz = extsz[t + 1 - charge[w]][0:1, :]
            szw = jnp.concatenate([sz] * LT, axis=1)
            rows = lax.broadcasted_iota(jnp.int32, (MS, MS), 0)
            cols = lax.broadcasted_iota(jnp.int32, (MS, MS), 1)
            hi, lo = split(jnp.where(rows < szw, rbuf[w, t], 0.0))
            r3[w, t, 0:MS, :] = hi
            r3[w, t, MS:2 * MS, :] = hi
            r3[w, t, 2 * MS:3 * MS, :] = lo
            hi, lo = split(jnp.where(cols < szw, lbuf[w, t], 0.0))
            for k in range(NCH):
                l3[t, k, :, w * 3 * CH:w * 3 * CH + CH] = hi[:, k * CH:(k + 1) * CH]
                l3[t, k, :, w * 3 * CH + CH:w * 3 * CH + 2 * CH] = hi[:, k * CH:(k + 1) * CH]
                l3[t, k, :, w * 3 * CH + 2 * CH:w * 3 * CH + 3 * CH] = lo[:, k * CH:(k + 1) * CH]
    for c in own + loads:
        c.wait()
    row_id = lax.broadcasted_iota(jnp.int32, (OWN, UNIT), 0) + term * OWN
    lane = lax.rem(lax.broadcasted_iota(jnp.int32, (OWN, UNIT), 1), MS)
    row_w = lax.broadcasted_iota(jnp.int32, (OWN, MS), 0) + term * OWN
    lane_w = lax.broadcasted_iota(jnp.int32, (OWN, MS), 1)
    for t in range(2):
        size = extsz[1 + t][0:1, 0:1]
        valid = (row_w < size) & (lane_w < size)
        for p in range(PH):
            stw[t, :, p * MS:(p + 1) * MS] = jnp.where(valid, stb[t, :, p, :], 0.0)
            inv[t, :, p * MS:(p + 1) * MS] = 1.0 / pcb[t, :, p, :].astype(F32)

    def contract(k, t):
        for w in range(2):
            slot = t + 1 - charge[w]
            for r in range(PH):
                for e in range(LT):
                    x = ext[k][slot, e, pl.ds(r, CH, stride=PH), :]
                    hi, lo = split(x)
                    lhs[r * CH:(r + 1) * CH, e * 128:(e + 1) * 128] = hi
                    lhs[r * CH:(r + 1) * CH, MS + e * 128:MS + (e + 1) * 128] = lo
                    lhs[r * CH:(r + 1) * CH, 2 * MS + e * 128:2 * MS + (e + 1) * 128] = hi
            zbuf[...] = jnp.dot(lhs[...], r3[w, t], preferred_element_type=F32)
            for e in range(LT):
                parts = [zbuf[r * CH:(r + 1) * CH, e * 128:(e + 1) * 128] for r in range(PH)]
                for p in range(PH):
                    z = ops[w, p, 0] * parts[0]
                    for r in range(1, PH):
                        z = z + ops[w, p, r] * parts[r]
                    hi, lo = split(z)
                    col = slice(p * MS + e * 128, p * MS + (e + 1) * 128)
                    rhs[w * 3 * CH:w * 3 * CH + CH, col] = hi
                    rhs[w * 3 * CH + CH:w * 3 * CH + 2 * CH, col] = lo
                    rhs[w * 3 * CH + 2 * CH:w * 3 * CH + 3 * CH, col] = hi
        for n in range(WIDE // 256):
            col = slice(n * 256, (n + 1) * 256)
            part = jnp.dot(l3[t, k], rhs[:, col], preferred_element_type=F32).reshape(8, 2, OWN, 256)
            if k == 0:
                acc[t, :, :, :, col] = part
            else:
                acc[t, :, :, :, col] += part

    def arrive(k):
        for d in range(2):
            @pl.when(can_get[d])
            def _():
                for e in range(LT):
                    halo(k, d, e).wait_recv()
                pass_on(k, d).start()
        for d in range(2):
            @pl.when(can_get[d])
            def _():
                pass_on(k, d).wait()

    for k in range(NCH - 1):
        arrive(k)

        def both(t, carry):
            contract(k, t)
            return carry

        lax.fori_loop(0, 2, both, 0)

    def swap(u):
        t, h = divmod(u, 2)
        return remote(acc.at[t, :, 1 - core, :, pl.ds(h * UNIT, UNIT)], prx.at[u], sem_p.at[0, u], sem_p.at[1, u], partner)

    def via(u, i):
        return remote(cs.at[u, yop * 2 + i], vrx.at[u, i], sem_v.at[0, u, i], sem_v.at[1, u, i], (up, down)[i])

    def direct(u, i, b):
        row = (yup, ydn)[i]
        return remote(cs.at[u, row * 2 + b], yrx.at[u, i, b], sem_y.at[0, u, i, b], sem_y.at[1, u, i, b], (up, down)[i])

    def across(u):
        return remote(ysb.at[u, 0], xrx.at[u], sem_x.at[0, u], sem_x.at[1, u], xpart)

    def s0(u):
        swap(u).start()

    def s1(u):
        t, h = divmod(u, 2)
        swap(u).wait_recv()
        for j in range(8):
            cs[u, j] = acc[t, j, core, :, h * UNIT:(h + 1) * UNIT] + prx[u, j]
        via(u, 0).start()
        via(u, 1).start()
        direct(u, 0, 1).start()
        direct(u, 1, 0).start()

    def s2(u):
        for i in range(2):
            via(u, i).wait_recv()
            row = (yup, ydn)[i]
            cs[u, row * 2 + i] += vrx[u, i]
            direct(u, i, i).start()

    def s3(u):
        for i in range(2):
            for b in range(2):
                direct(u, i, b).wait_recv()
        for q, b in ((0, 1 - xh), (1, xh)):
            ysb[u, q] = cs[u, y * 2 + b] + yrx[u, 0, b] + yrx[u, 1, b]
            if q == 0:
                across(u).start()

    def s4(u):
        t, h = divmod(u, 2)
        across(u).wait_recv()
        col = slice(h * UNIT, (h + 1) * UNIT)
        s = stw[t, :, col]
        valid = (row_id < extsz[1 + t][0:1, 0:1]) & (lane < extsz[1 + t][0:1, 0:1])
        img[t, :, col] = jnp.where(valid, ysb[u, 1] + xrx[u] + energy[t] * s, 0.0)

    last = NCH - 1
    arrive(last)
    contract(last, 0)
    s0(0)
    s0(1)
    s1(0)
    s1(1)
    contract(last, 1)
    s0(2)
    s0(3)
    s2(0)
    s1(2)
    s2(1)
    s1(3)
    s3(0)
    s2(2)
    s3(1)
    s2(3)
    s4(0)
    s3(2)
    s4(1)
    s3(3)
    s4(2)
    s4(3)

    def total_of(x):
        x = jnp.sum(x, axis=0)
        return jnp.sum(jnp.sum(x, axis=0, keepdims=True), axis=1, keepdims=True)

    s, g, q = stw[...], img[...], inv[...]
    w_sum, c_sum = total_of(s * s), total_of(s * g)
    shift = jnp.where(w_sum > 0.0, c_sum / jnp.where(w_sum > 0.0, w_sum, 1.0), 0.0)
    m, v = s - (g - shift * s) * q, s * q
    a_sum, b_sum, d_sum = total_of(m * m), total_of(m * v), total_of(v * v)

    number = term * 8 + sec
    sub8 = lax.broadcasted_iota(jnp.int32, (8, 128), 0)
    lane8 = lax.broadcasted_iota(jnp.int32, (8, 128), 1)
    table = jnp.zeros((8, 128), F32)
    for i, v in enumerate((c_sum, w_sum, a_sum, b_sum, d_sum, shift)):
        table = jnp.where(sub8 == i, v, table)
    table = jnp.where(lane8 == number, table, 0.0)
    gt[0] = table

    def to_a(i):
        return remote(gt.at[0], ga.at[me_a], sem_ga.at[0, i], sem_ga.at[1, me_a], peer_a(i))

    def from_a(i):
        return remote(gt.at[0], ga.at[i], sem_ga.at[0, i], sem_ga.at[1, i], peer_a(i))

    def to_b(i):
        return remote(gt.at[1], gb.at[me_b], sem_gb.at[0, i], sem_gb.at[1, me_b], peer_b(i))

    def from_b(i):
        return remote(gt.at[1], gb.at[i], sem_gb.at[0, i], sem_gb.at[1, i], peer_b(i))

    for o in range(1, 8):
        to_a(lax.rem(me_a + o, 8)).start()
    for o in range(1, 8):
        i = lax.rem(me_a + o, 8)
        from_a(i).wait_recv()
        table = table + ga[i]
    gt[1] = table
    for o in range(1, 16):
        to_b(lax.rem(me_b + o, 16)).start()
    for o in range(1, 16):
        i = lax.rem(me_b + o, 16)
        from_b(i).wait_recv()
        table = table + gb[i]

    def row_sum(x):
        return jnp.sum(x, axis=1, keepdims=True)

    e_all = row_sum(table[0:1]) / row_sum(table[1:2])
    de = e_all - table[5:6]
    square = row_sum(table[2:3] + (2.0 * table[3:4] + de * table[4:5]) * de)
    scale = lax.rsqrt(square / (16.0 * MS * WIDE) + EPSILON)
    for t in range(2):
        for p in range(PH):
            col = slice(p * MS, (p + 1) * MS)
            s = stw[t, :, col]
            out[t, :, p, :] = (s - (img[t, :, col] - e_all * s) * inv[t, :, col]) * scale
    eng[0] = jnp.sum(e_all)

    for d in range(2):
        @pl.when(can_send[d])
        def _():
            for k in range(NCH):
                for e in range(LT):
                    halo(k, d, e).wait_send()
    for u in range(4):
        swap(u).wait_send()
        for i in range(2):
            via(u, i).wait_send()
            for b in range(2):
                direct(u, i, b).wait_send()
        across(u).wait_send()
    for o in range(1, 8):
        to_a(lax.rem(me_a + o, 8)).wait_send()
    for o in range(1, 16):
        to_b(lax.rem(me_b + o, 16)).wait_send()


def body(psi, precond, left, right, ops, charge, sizes, energy):
    vm = pl.BlockSpec(memory_space=pltpu.VMEM)
    sm = pl.BlockSpec(memory_space=pltpu.SMEM)
    anyw = pl.BlockSpec(memory_space=pl.ANY)
    dma = pltpu.SemaphoreType.DMA
    return pl.pallas_call(
        kernel,
        out_shape=(
            jax.ShapeDtypeStruct((2, OWN, PH, MS), F32),
            jax.ShapeDtypeStruct((1,), F32),
        ),
        in_specs=[anyw, anyw, anyw, anyw, sm, sm, sm, sm],
        out_specs=(vm, sm),
        scratch_shapes=[
            pltpu.VMEM((4, LT, CH * PH, 128), F32),
            pltpu.VMEM((4, LT, CH * PH, 128), F32),
            pltpu.VMEM((4, LT, CH * PH, 128), F32),
            pltpu.VMEM((4, 8, 128), jnp.int32),
            pltpu.VMEM((2, 8, 128), jnp.int32),
            pltpu.VMEM((2, 2, MS, MS), F32),
            pltpu.VMEM((2, 2, MS, MS), F32),
            pltpu.VMEM((2, NCH, MS, 6 * CH), BF16),
            pltpu.VMEM((2, 2, 3 * MS, MS), BF16),
            pltpu.VMEM((PH * CH, 3 * MS), BF16),
            pltpu.VMEM((PH * CH, MS), F32),
            pltpu.VMEM((6 * CH, WIDE), BF16),
            pltpu.VMEM((2, 8, 2, OWN, WIDE), F32),
            pltpu.VMEM((4, 8, OWN, UNIT), F32),
            pltpu.VMEM((4, 8, OWN, UNIT), F32),
            pltpu.VMEM((4, 2, OWN, UNIT), F32),
            pltpu.VMEM((4, 2, 2, OWN, UNIT), F32),
            pltpu.VMEM((4, 2, OWN, UNIT), F32),
            pltpu.VMEM((4, OWN, UNIT), F32),
            pltpu.VMEM((2, OWN, PH, MS), F32),
            pltpu.VMEM((2, OWN, PH, MS), BF16),
            pltpu.VMEM((2, OWN, WIDE), F32),
            pltpu.VMEM((2, OWN, WIDE), F32),
            pltpu.VMEM((2, OWN, WIDE), F32),
            pltpu.VMEM((8, 8, 128), F32),
            pltpu.VMEM((16, 8, 128), F32),
            pltpu.VMEM((2, 8, 128), F32),
            dma((NCH, 2, LT)),
            dma((2,)),
            dma((2,)),
            dma((2, NCH, 2, LT)),
            dma((2, NCH, 2)),
            dma((2, 2)),
            dma((2, 4)),
            dma((2, 4, 2)),
            dma((2, 4, 2, 2)),
            dma((2, 4)),
            dma((2, 8)),
            dma((2, 16)),
        ],
        compiler_params=pltpu.CompilerParams(
            collective_id=0, has_side_effects=True, vmem_limit_bytes=60 * 1024 * 1024
        ),
        name="update",
    )(psi, precond, left, right, ops, charge, sizes, energy)


def solution(mesh):
    in_specs = (
        P("sector", None, None, None),
        P("sector", None, None, None),
        P("term", "sector", None, None),
        P("term", "sector", None, None),
        P("term", None, None),
        P("term"),
        P("sector"),
        P("sector"),
    )
    out_specs = (P("sector", "term", None, None), P())
    return jax.shard_map(body, mesh=mesh, in_specs=in_specs, out_specs=out_specs, check_vma=False)
```

```python
import jax
import jax.numpy as jnp
from jax import lax
from jax.experimental import pallas as pl
from jax.experimental.pallas import tpu as pltpu
from jax.sharding import PartitionSpec as P

EPSILON = 1e-06
F32 = jnp.float32
BF16 = jnp.bfloat16
MS = 384
PH = 4
WPAD = 512
CH = 128
NCH = MS // CH
NW = 4
STRAIGHT = (96, 0, 0)
PIECE = (36, 48, 48)
OWN = MS // 16
WIDE = PH * MS
UNIT = MS
NU = WIDE // UNIT


def split(x):
    hi = x.astype(BF16)
    return hi, (x - hi.astype(F32)).astype(BF16)


def kernel(
    psi, precond, lenv, renv, ops, charge, sizes, energy,
    out, eng,
    ext0, ext1, ext2, extsz, szt, opv, cht, chs, lbuf, rbuf, l3, r3, sx, zbuf, x2, acc,
    vrx, yrx, ysb, xrx, fin, prx, stb, pcb, stw, inv, msk, img, ga, gb, gt,
    sem_in, sem_own, sem_lr, sem_er, sem_zq, sem_zd, sem_r, sem_sz, sem_cs, sem_v, sem_y, sem_x, sem_p, sem_ga, sem_gb,
):
    ext = (ext0, ext1, ext2)
    term = lax.axis_index("term")
    sec = lax.axis_index("sector")
    y = lax.div(term, 4)
    xh = lax.rem(lax.div(term, 2), 2)
    core = lax.rem(term, 2)
    other = 1 - core

    def dev(yy, hh, cc, ss=None):
        return {"term": yy * 4 + hh * 2 + cc, "sector": sec if ss is None else ss}

    partner = dev(y, xh, other)
    yup, ydn, yop = lax.rem(y + 1, 4), lax.rem(y + 3, 4), lax.rem(y + 2, 4)
    up, down = dev(yup, xh, core), dev(ydn, xh, core)
    xpart = dev(y, 1 - xh, core)
    ahead = dev(y, xh, core, lax.rem(sec + 1 + 6 * core, 8))
    edge = sec == 7 * core

    me_a = y * 2 + core
    me_b = xh * 8 + sec

    def peer_a(i):
        return dev(lax.div(i, 2), xh, lax.rem(i, 2))

    def peer_b(i):
        return dev(y, lax.div(i, 8), core, lax.rem(i, 8))

    def rows_of(ref, first, n):
        return ref.at[pl.ds(pl.multiple_of(first * PH, 8), n * PH), :].reshape(n, PH, 128)

    own = [
        pltpu.make_async_copy(psi.at[:, pl.ds(term * OWN, OWN)], stb, sem_own.at[0]),
        pltpu.make_async_copy(precond.at[:, pl.ds(term * OWN, OWN)], pcb, sem_own.at[1]),
    ]
    envs = [
        pltpu.make_async_copy(renv.at[:, core], rbuf.at[pl.ds(0, 2)], sem_lr.at[0]),
        pltpu.make_async_copy(lenv.at[:, core], lbuf.at[pl.ds(0, 2)], sem_lr.at[1]),
    ]
    loads = []
    for k in range(NCH):
        for s in range(2):
            loads.append(pltpu.make_async_copy(
                psi.at[s, :, :, pl.ds(k * CH, CH)], rows_of(ext[k].at[1 + s], 0, MS), sem_in.at[k, s]))

    barrier = pltpu.get_barrier_semaphore()
    for o in range(1, 16):
        pl.semaphore_signal(barrier, inc=1, device_id=peer_b(lax.rem(me_b + o, 16)), device_id_type=pl.DeviceIdType.MESH)
    for o in range(1, 8):
        pl.semaphore_signal(barrier, inc=1, device_id=peer_a(lax.rem(me_a + o, 8)), device_id_type=pl.DeviceIdType.MESH)
    for c in own + envs + loads:
        c.start()

    for s in range(2):
        szt[s] = jnp.full((8, 128), sizes[s], jnp.int32)
        extsz[1 + s] = jnp.full((8, 128), sizes[s], jnp.int32)
    for w in range(2):
        cht[0, w] = jnp.full((8, 128), charge[w], jnp.int32)
        for p in range(PH):
            for r in range(PH):
                i = w * 16 + p * PH + r
                opv[i:i + 1, :] = jnp.full((1, 128), ops[w, p, r], F32)

    row_w = lax.broadcasted_iota(jnp.int32, (OWN, MS), 0) + term * OWN
    lane_w = lax.broadcasted_iota(jnp.int32, (OWN, MS), 1)
    for c in own:
        c.wait()
    for t in range(2):
        size = sizes[t]
        valid = (row_w < size) & (lane_w < size)
        mask = jnp.where(valid, 1.0, 0.0)
        for p in range(PH):
            msk[t, :, p * MS:(p + 1) * MS] = mask
            stw[t, :, p * MS:(p + 1) * MS] = jnp.where(valid, stb[t, :, p, :], 0.0)
            inv[t, :, p * MS:(p + 1) * MS] = 1.0 / pcb[t, :, p, :].astype(F32)

    pl.semaphore_wait(barrier, 22)

    def remote(src, dst, s, r, where):
        return pltpu.make_async_remote_copy(
            src_ref=src, dst_ref=dst, send_sem=s, recv_sem=r, device_id=where, device_id_type=pl.DeviceIdType.MESH)

    def halo(k, first, n, sem, *i):
        return remote(
            psi.at[other, pl.ds(first, n), :, pl.ds(k * CH, CH)],
            rows_of(ext[k].at[0], first, n), sem.at[(0, k) + i], sem.at[(1, k) + i], ahead)

    def start_of(k, i):
        return STRAIGHT[k] + (lax.rem(y, 2) * 4 + i) * PIECE[k]

    def piece(k, i):
        return halo(k, start_of(k, i), PIECE[k], sem_zq, i)

    def straight(k):
        return halo(k, 0, STRAIGHT[k], sem_zd)

    def relay(k, i):
        ref = ext[k].at[0, pl.ds(pl.multiple_of(start_of(k, i) * PH, 8), PIECE[k] * PH), :]
        return remote(ref, ref, sem_r.at[0, k, i], sem_r.at[1, k, i], (up, down)[i % 2])

    size_copy = remote(szt.at[other], extsz.at[0], sem_sz.at[0], sem_sz.at[1], ahead)
    charge_copy = remote(cht.at[0], cht.at[1], sem_cs.at[0, 0], sem_cs.at[1, 0], partner)
    ops_copy = remote(opv.at[pl.ds(0, 32)], opv.at[pl.ds(32, 32)], sem_cs.at[0, 1], sem_cs.at[1, 1], partner)
    r_copy = remote(renv.at[:, other], rbuf.at[pl.ds(2, 2)], sem_er.at[0, 0], sem_er.at[1, 0], partner)
    l_copy = remote(lenv.at[:, other], lbuf.at[pl.ds(2, 2)], sem_er.at[0, 1], sem_er.at[1, 1], partner)

    size_copy.start()
    charge_copy.start()
    ops_copy.start()
    for k in range(NCH):
        for i in range(4):
            piece(k, i).start()
        if STRAIGHT[k]:
            straight(k).start()
        if k == 0:
            l_copy.start()
            r_copy.start()
    r3[:, :, MS:WPAD] = jnp.zeros((NCH, NW * 3 * CH, WPAD - MS), BF16)

    size_copy.wait_recv()
    extsz[0] = jnp.where(edge, 0, extsz[0])
    row_m = lax.broadcasted_iota(jnp.int32, (MS, MS), 0)
    col_m = lax.broadcasted_iota(jnp.int32, (MS, MS), 1)

    def slot_of(c):
        rel = core - c
        return jnp.where((rel < 0) | (rel > 1), 0, rel + 1)

    def set_right(w, slot):
        size = jnp.concatenate([extsz[slot][0:1, :]] * NCH, axis=1)
        hi, lo = split(jnp.where(row_m < size, rbuf[w], 0.0))
        for k in range(NCH):
            cut = slice(k * CH, (k + 1) * CH)
            base = w * 3 * CH
            r3[k, base:base + CH, 0:MS] = hi[cut]
            r3[k, base + CH:base + 2 * CH, 0:MS] = hi[cut]
            r3[k, base + 2 * CH:base + 3 * CH, 0:MS] = lo[cut]

    def set_left(w, slot):
        size = jnp.concatenate([extsz[slot][0:1, :]] * NCH, axis=1)
        hi, lo = split(jnp.where(col_m < size, lbuf[w], 0.0))
        l3[w, :, 0:MS] = hi
        l3[w, :, MS:2 * MS] = hi
        l3[w, :, 2 * MS:3 * MS] = lo

    slots = [slot_of(charge[0]), slot_of(charge[1])]
    envs[1].wait()
    set_left(0, slots[0])

    def pass_on(k, i):
        piece(k, i).wait_recv()
        relay(k, i).start()

    def arrive(k):
        if STRAIGHT[k]:
            straight(k).wait_recv()
        for i in range(4):
            relay(k, i).wait_recv()

    pass_on(0, 0)
    set_left(1, slots[1])
    pass_on(0, 1)
    charge_copy.wait_recv()
    to_smem = pltpu.make_async_copy(cht.at[1, :, 0, :], chs, sem_lr.at[2])
    to_smem.start()
    to_smem.wait()
    slots += [slot_of(chs[0, 0]), slot_of(chs[1, 0])]
    pass_on(0, 2)
    envs[0].wait()
    set_right(0, slots[0])
    pass_on(0, 3)
    set_right(1, slots[1])
    l_copy.wait_recv()
    set_left(2, slots[2])
    set_left(3, slots[3])
    r_copy.wait_recv()
    set_right(2, slots[2])
    set_right(3, slots[3])
    ops_copy.wait_recv()
    for c in loads:
        c.wait()

    def prepare(k, w):
        b = w % 2
        for r in range(PH):
            col = slice(r * CH, (r + 1) * CH)
            for first in range(0, MS, 128):
                hi, lo = split(ext[k][slots[w], pl.ds(first * PH + r, 128, stride=PH), :])
                sx[b, first:first + 128, col] = hi
                sx[b, MS + first:MS + first + 128, col] = lo
                sx[b, 2 * MS + first:2 * MS + first + 128, col] = hi

    def stage1(k, w):
        b = w % 2
        zbuf[b] = jnp.dot(l3[w], sx[b], preferred_element_type=F32)
        step = 32
        for first in range(0, MS, step):
            parts = [zbuf[b, first:first + step, r * CH:(r + 1) * CH] for r in range(PH)]
            for p in range(PH):
                i = w * 16 + p * PH
                z = opv[i:i + 1, :] * parts[0]
                for r in range(1, PH):
                    z = z + opv[i + r:i + r + 1, :] * parts[r]
                hi, lo = split(z)
                rows = slice(p * MS + first, p * MS + first + step)
                base = w * 3 * CH
                x2[k % 2, rows, base:base + CH] = hi
                x2[k % 2, rows, base + CH:base + 2 * CH] = lo
                x2[k % 2, rows, base + 2 * CH:base + 3 * CH] = hi

    def stage2(k, p):
        part = jnp.dot(x2[k % 2, p * MS:(p + 1) * MS, :], r3[k], preferred_element_type=F32)
        part = part[:, 0:MS].reshape(4, 2, 2, OWN, MS)
        if k == 0:
            acc[p] = part
        else:
            acc[p] += part

    def via(u, i):
        return remote(acc.at[u, yop, i], vrx.at[u, i], sem_v.at[0, u, i], sem_v.at[1, u, i], (up, down)[i])

    def direct(u, i, b):
        return remote(
            acc.at[u, (yup, ydn)[i], b], yrx.at[u, i, b],
            sem_y.at[0, u, i, b], sem_y.at[1, u, i, b], (up, down)[i])

    def across(u):
        return remote(ysb.at[u, 0], xrx.at[u], sem_x.at[0, u], sem_x.at[1, u], xpart)

    def swap(u):
        return remote(fin.at[u, other], prx.at[u], sem_p.at[0, u], sem_p.at[1, u], partner)

    def s1(u):
        via(u, 0).start()
        via(u, 1).start()
        direct(u, 0, 1).start()
        direct(u, 1, 0).start()

    def s2(u):
        for i in range(2):
            via(u, i).wait_recv()
            acc[u, (yup, ydn)[i], i] += vrx[u, i]
            direct(u, i, i).start()

    def s3(u):
        for i in range(2):
            for b in range(2):
                direct(u, i, b).wait_recv()
        for q, b in ((0, 1 - xh), (1, xh)):
            ysb[u, q] = acc[u, y, b] + yrx[u, 0, b] + yrx[u, 1, b]
            if q == 0:
                across(u).start()

    def s4(u):
        across(u).wait_recv()
        fin[u] = ysb[u, 1] + xrx[u]
        swap(u).start()

    def s5(u):
        swap(u).wait_recv()
        col = slice(u * UNIT, (u + 1) * UNIT)
        for t, total in ((core, fin[u, core]), (other, prx[u])):
            img[t, :, col] = (total + energy[t] * stw[t, :, col]) * msk[t, :, col]

    last = NCH - 1
    for k in range(NCH):
        if k == 1:
            pass_on(2, 0)
            pass_on(2, 1)
        arrive(k)
        for w in range(NW):
            prepare(k, w)
            stage1(k, w)
            if k == 0:
                pass_on(1, w)
            if k == 1 and w < 2:
                pass_on(2, w + 2)
        for p in range(PH):
            stage2(k, p)
            if k == last and p < 2:
                s1(p)
    s2(0)
    s1(2)
    s2(1)
    s1(3)
    s2(2)
    s3(0)
    s2(3)
    s3(1)
    s4(0)
    s3(2)
    s4(1)
    s5(0)
    s3(3)
    s4(2)
    s5(1)
    s4(3)
    s5(2)
    s5(3)

    def total_of(x):
        x = jnp.sum(x, axis=0)
        return jnp.sum(jnp.sum(x, axis=0, keepdims=True), axis=1, keepdims=True)

    s, g, q = stw[...], img[...], inv[...]
    w_sum, c_sum = total_of(s * s), total_of(s * g)
    shift = jnp.where(w_sum > 0.0, c_sum / jnp.where(w_sum > 0.0, w_sum, 1.0), 0.0)
    m, v = s - (g - shift * s) * q, s * q
    a_sum, b_sum, d_sum = total_of(m * m), total_of(m * v), total_of(v * v)

    number = term * 8 + sec
    sub8 = lax.broadcasted_iota(jnp.int32, (8, 128), 0)
    lane8 = lax.broadcasted_iota(jnp.int32, (8, 128), 1)
    table = jnp.zeros((8, 128), F32)
    for i, v in enumerate((c_sum, w_sum, a_sum, b_sum, d_sum, shift)):
        table = jnp.where(sub8 == i, v, table)
    table = jnp.where(lane8 == number, table, 0.0)
    gt[0] = table

    def to_a(i):
        return remote(gt.at[0], ga.at[me_a], sem_ga.at[0, i], sem_ga.at[1, me_a], peer_a(i))

    def from_a(i):
        return remote(gt.at[0], ga.at[i], sem_ga.at[0, i], sem_ga.at[1, i], peer_a(i))

    def to_b(i):
        return remote(gt.at[1], gb.at[me_b], sem_gb.at[0, i], sem_gb.at[1, me_b], peer_b(i))

    def from_b(i):
        return remote(gt.at[1], gb.at[i], sem_gb.at[0, i], sem_gb.at[1, i], peer_b(i))

    for o in range(1, 8):
        to_a(lax.rem(me_a + o, 8)).start()
    for o in range(1, 8):
        i = lax.rem(me_a + o, 8)
        from_a(i).wait_recv()
        table = table + ga[i]
    gt[1] = table
    for o in range(1, 16):
        to_b(lax.rem(me_b + o, 16)).start()
    for o in range(1, 16):
        i = lax.rem(me_b + o, 16)
        from_b(i).wait_recv()
        table = table + gb[i]

    def row_sum(x):
        return jnp.sum(x, axis=1, keepdims=True)

    e_all = row_sum(table[0:1]) / row_sum(table[1:2])
    de = e_all - table[5:6]
    square = row_sum(table[2:3] + (2.0 * table[3:4] + de * table[4:5]) * de)
    scale = lax.rsqrt(square / (16.0 * MS * WIDE) + EPSILON)
    for t in range(2):
        for p in range(PH):
            col = slice(p * MS, (p + 1) * MS)
            s = stw[t, :, col]
            out[t, :, p, :] = (s - (img[t, :, col] - e_all * s) * inv[t, :, col]) * scale
    eng[0] = jnp.sum(e_all)

    for c in (size_copy, charge_copy, ops_copy, r_copy, l_copy):
        c.wait_send()
    for k in range(NCH):
        for i in range(4):
            piece(k, i).wait_send()
        if STRAIGHT[k]:
            straight(k).wait_send()
        for i in range(4):
            relay(k, i).wait_send()
    for u in range(NU):
        for i in range(2):
            via(u, i).wait_send()
            for b in range(2):
                direct(u, i, b).wait_send()
        across(u).wait_send()
        swap(u).wait_send()
    for o in range(1, 8):
        to_a(lax.rem(me_a + o, 8)).wait_send()
    for o in range(1, 16):
        to_b(lax.rem(me_b + o, 16)).wait_send()


def body(psi, precond, left, right, ops, charge, sizes, energy):
    vm = pl.BlockSpec(memory_space=pltpu.VMEM)
    sm = pl.BlockSpec(memory_space=pltpu.SMEM)
    anyw = pl.BlockSpec(memory_space=pl.ANY)
    dma = pltpu.SemaphoreType.DMA
    return pl.pallas_call(
        kernel,
        out_shape=(
            jax.ShapeDtypeStruct((2, OWN, PH, MS), F32),
            jax.ShapeDtypeStruct((1,), F32),
        ),
        in_specs=[anyw, anyw, anyw, anyw, sm, sm, sm, sm],
        out_specs=(vm, sm),
        scratch_shapes=[
            pltpu.VMEM((3, MS * PH, CH), F32),
            pltpu.VMEM((3, MS * PH, CH), F32),
            pltpu.VMEM((3, MS * PH, CH), F32),
            pltpu.VMEM((3, 8, 128), jnp.int32),
            pltpu.VMEM((2, 8, 128), jnp.int32),
            pltpu.VMEM((64, 128), F32),
            pltpu.VMEM((2, 2, 8, 128), jnp.int32),
            pltpu.SMEM((2, 128), jnp.int32),
            pltpu.VMEM((NW, MS, MS), F32),
            pltpu.VMEM((NW, MS, MS), F32),
            pltpu.VMEM((NW, MS, 3 * MS), BF16),
            pltpu.VMEM((NCH, NW * 3 * CH, WPAD), BF16),
            pltpu.VMEM((2, 3 * MS, PH * CH), BF16),
            pltpu.VMEM((2, MS, PH * CH), F32),
            pltpu.VMEM((2, PH * MS, NW * 3 * CH), BF16),
            pltpu.VMEM((PH, 4, 2, 2, OWN, MS), F32),
            pltpu.VMEM((NU, 2, 2, OWN, UNIT), F32),
            pltpu.VMEM((NU, 2, 2, 2, OWN, UNIT), F32),
            pltpu.VMEM((NU, 2, 2, OWN, UNIT), F32),
            pltpu.VMEM((NU, 2, OWN, UNIT), F32),
            pltpu.VMEM((NU, 2, OWN, UNIT), F32),
            pltpu.VMEM((NU, OWN, UNIT), F32),
            pltpu.VMEM((2, OWN, PH, MS), F32),
            pltpu.VMEM((2, OWN, PH, MS), BF16),
            pltpu.VMEM((2, OWN, WIDE), F32),
            pltpu.VMEM((2, OWN, WIDE), F32),
            pltpu.VMEM((2, OWN, WIDE), F32),
            pltpu.VMEM((2, OWN, WIDE), F32),
            pltpu.VMEM((8, 8, 128), F32),
            pltpu.VMEM((16, 8, 128), F32),
            pltpu.VMEM((2, 8, 128), F32),
            dma((NCH, 2)),
            dma((2,)),
            dma((3,)),
            dma((2, 2)),
            dma((2, NCH, 4)),
            dma((2, NCH)),
            dma((2, NCH, 4)),
            dma((2,)),
            dma((2, 2)),
            dma((2, NU, 2)),
            dma((2, NU, 2, 2)),
            dma((2, NU)),
            dma((2, NU)),
            dma((2, 8)),
            dma((2, 16)),
        ],
        compiler_params=pltpu.CompilerParams(
            collective_id=0, has_side_effects=True, vmem_limit_bytes=60 * 1024 * 1024
        ),
        name="update",
    )(psi, precond, left, right, ops, charge, sizes, energy)


def solution(mesh):
    in_specs = (
        P("sector", None, None, None),
        P("sector", None, None, None),
        P("term", "sector", None, None),
        P("term", "sector", None, None),
        P("term", None, None),
        P("term"),
        P("sector"),
        P("sector"),
    )
    out_specs = (P("sector", "term", None, None), P())
    return jax.shard_map(body, mesh=mesh, in_specs=in_specs, out_specs=out_specs, check_vma=False)
```

```python
import jax
import jax.numpy as jnp
from jax import lax
from jax.experimental import pallas as pl
from jax.experimental.pallas import tpu as pltpu
from jax.sharding import PartitionSpec as P

EPSILON = 1e-06
F32 = jnp.float32
BF16 = jnp.bfloat16
MS = 384
PH = 4
WPAD = 512
CH = 128
NCH = MS // CH
NW = 4
STRAIGHT = (192, 192, 192)
PIECE = (48, 48, 48)
OWN = MS // 16
WIDE = PH * MS
UNIT = MS
NU = WIDE // UNIT


def split(x):
    hi = x.astype(BF16)
    return hi, (x - hi.astype(F32)).astype(BF16)


def kernel(
    psi, precond, lenv, renv, ops, charge, sizes, energy,
    out, eng,
    ext0, ext1, ext2, extsz, szt, opv, cht, chs, lbuf, rbuf, l3, r3, sx, zbuf, x2, acc,
    vrx, yrx, ysb, xrx, vrf, yrf, xrf, fin, prx, stb, pcb, stw, inv, msk, img, ga, gb, gt,
    sem_in, sem_own, sem_lr, sem_er, sem_zq, sem_zd, sem_r, sem_sz, sem_cs, sem_v, sem_y, sem_x, sem_xf, sem_p, sem_ga, sem_gb,
):
    ext = (ext0, ext1, ext2)
    term = lax.axis_index("term")
    sec = lax.axis_index("sector")
    y = lax.div(term, 4)
    xh = lax.rem(lax.div(term, 2), 2)
    core = lax.rem(term, 2)
    other = 1 - core

    def dev(yy, hh, cc, ss=None):
        return {"term": yy * 4 + hh * 2 + cc, "sector": sec if ss is None else ss}

    partner = dev(y, xh, other)
    yup, ydn, yop = lax.rem(y + 1, 4), lax.rem(y + 3, 4), lax.rem(y + 2, 4)
    up, down = dev(yup, xh, core), dev(ydn, xh, core)
    xpart, xdiag = dev(y, 1 - xh, core), dev(y, 1 - xh, other)
    ahead = dev(y, xh, core, lax.rem(sec + 1 + 6 * core, 8))
    edge = sec == 7 * core

    me_a = y * 2 + core
    me_b = xh * 8 + sec

    def peer_a(i):
        return dev(lax.div(i, 2), xh, lax.rem(i, 2))

    def peer_b(i):
        return dev(y, lax.div(i, 8), core, lax.rem(i, 8))

    def rows_of(ref, first, n):
        return ref.at[pl.ds(pl.multiple_of(first * PH, 8), n * PH), :].reshape(n, PH, 128)

    own = [
        pltpu.make_async_copy(psi.at[:, pl.ds(term * OWN, OWN)], stb, sem_own.at[0]),
        pltpu.make_async_copy(precond.at[:, pl.ds(term * OWN, OWN)], pcb, sem_own.at[1]),
    ]
    envs = [
        pltpu.make_async_copy(renv.at[:, core], rbuf.at[pl.ds(0, 2)], sem_lr.at[0]),
        pltpu.make_async_copy(lenv.at[:, core], lbuf.at[pl.ds(0, 2)], sem_lr.at[1]),
    ]
    loads = []
    for k in range(NCH):
        for s in range(2):
            loads.append(pltpu.make_async_copy(
                psi.at[s, :, :, pl.ds(k * CH, CH)], rows_of(ext[k].at[1 + s], 0, MS), sem_in.at[k, s]))

    barrier = pltpu.get_barrier_semaphore()
    for o in range(1, 16):
        pl.semaphore_signal(barrier, inc=1, device_id=peer_b(lax.rem(me_b + o, 16)), device_id_type=pl.DeviceIdType.MESH)
    for o in range(1, 8):
        pl.semaphore_signal(barrier, inc=1, device_id=peer_a(lax.rem(me_a + o, 8)), device_id_type=pl.DeviceIdType.MESH)
    pl.semaphore_signal(barrier, inc=1, device_id=xdiag, device_id_type=pl.DeviceIdType.MESH)
    for c in own + envs + loads:
        c.start()

    for s in range(2):
        szt[s] = jnp.full((8, 128), sizes[s], jnp.int32)
        extsz[1 + s] = jnp.full((8, 128), sizes[s], jnp.int32)
    for w in range(2):
        cht[0, w] = jnp.full((8, 128), charge[w], jnp.int32)
        for p in range(PH):
            for r in range(PH):
                i = w * 16 + p * PH + r
                opv[i:i + 1, :] = jnp.full((1, 128), ops[w, p, r], F32)

    row_w = lax.broadcasted_iota(jnp.int32, (OWN, MS), 0) + term * OWN
    lane_w = lax.broadcasted_iota(jnp.int32, (OWN, MS), 1)
    for c in own:
        c.wait()
    for t in range(2):
        size = sizes[t]
        valid = (row_w < size) & (lane_w < size)
        mask = jnp.where(valid, 1.0, 0.0)
        for p in range(PH):
            msk[t, :, p * MS:(p + 1) * MS] = mask
            stw[t, :, p * MS:(p + 1) * MS] = jnp.where(valid, stb[t, :, p, :], 0.0)
            inv[t, :, p * MS:(p + 1) * MS] = 1.0 / pcb[t, :, p, :].astype(F32)

    pl.semaphore_wait(barrier, 23)

    def remote(src, dst, s, r, where):
        return pltpu.make_async_remote_copy(
            src_ref=src, dst_ref=dst, send_sem=s, recv_sem=r, device_id=where, device_id_type=pl.DeviceIdType.MESH)

    def halo(k, first, n, sem, *i):
        return remote(
            psi.at[other, pl.ds(first, n), :, pl.ds(k * CH, CH)],
            rows_of(ext[k].at[0], first, n), sem.at[(0, k) + i], sem.at[(1, k) + i], ahead)

    def start_of(k, i):
        return STRAIGHT[k] + (lax.rem(y, 2) * 2 + i) * PIECE[k]

    def piece(k, i):
        return halo(k, start_of(k, i), PIECE[k], sem_zq, i)

    def straight(k):
        return halo(k, 0, STRAIGHT[k], sem_zd)

    def relay(k, i):
        ref = ext[k].at[0, pl.ds(pl.multiple_of(start_of(k, i) * PH, 8), PIECE[k] * PH), :]
        return remote(ref, ref, sem_r.at[0, k, i], sem_r.at[1, k, i], (up, down)[i])

    size_copy = remote(szt.at[other], extsz.at[0], sem_sz.at[0], sem_sz.at[1], ahead)
    charge_copy = remote(cht.at[0], cht.at[1], sem_cs.at[0, 0], sem_cs.at[1, 0], partner)
    ops_copy = remote(opv.at[pl.ds(0, 32)], opv.at[pl.ds(32, 32)], sem_cs.at[0, 1], sem_cs.at[1, 1], partner)
    r_copy = remote(renv.at[:, other], rbuf.at[pl.ds(2, 2)], sem_er.at[0, 0], sem_er.at[1, 0], partner)
    l_copy = remote(lenv.at[:, other], lbuf.at[pl.ds(2, 2)], sem_er.at[0, 1], sem_er.at[1, 1], partner)

    size_copy.start()
    charge_copy.start()
    ops_copy.start()
    for k in range(NCH):
        for i in range(2):
            piece(k, i).start()
        if STRAIGHT[k]:
            straight(k).start()
        if k == 0:
            l_copy.start()
            r_copy.start()
    r3[:, :, MS:WPAD] = jnp.zeros((NCH, NW * 3 * CH, WPAD - MS), BF16)

    size_copy.wait_recv()
    extsz[0] = jnp.where(edge, 0, extsz[0])
    row_m = lax.broadcasted_iota(jnp.int32, (MS, MS), 0)
    col_m = lax.broadcasted_iota(jnp.int32, (MS, MS), 1)

    def slot_of(c):
        rel = core - c
        return jnp.where((rel < 0) | (rel > 1), 0, rel + 1)

    def set_right(w, slot):
        size = jnp.concatenate([extsz[slot][0:1, :]] * NCH, axis=1)
        hi, lo = split(jnp.where(row_m < size, rbuf[w], 0.0))
        for k in range(NCH):
            cut = slice(k * CH, (k + 1) * CH)
            base = w * 3 * CH
            r3[k, base:base + CH, 0:MS] = hi[cut]
            r3[k, base + CH:base + 2 * CH, 0:MS] = hi[cut]
            r3[k, base + 2 * CH:base + 3 * CH, 0:MS] = lo[cut]

    def set_left(w, slot):
        size = jnp.concatenate([extsz[slot][0:1, :]] * NCH, axis=1)
        hi, lo = split(jnp.where(col_m < size, lbuf[w], 0.0))
        l3[w, :, 0:MS] = hi
        l3[w, :, MS:2 * MS] = hi
        l3[w, :, 2 * MS:3 * MS] = lo

    slots = [slot_of(charge[0]), slot_of(charge[1])]
    envs[1].wait()
    set_left(0, slots[0])

    def pass_on(k, i):
        piece(k, i).wait_recv()
        relay(k, i).start()

    def arrive(k):
        if STRAIGHT[k]:
            straight(k).wait_recv()
        for i in range(2):
            relay(k, i).wait_recv()

    pass_on(0, 0)
    set_left(1, slots[1])
    pass_on(0, 1)
    charge_copy.wait_recv()
    to_smem = pltpu.make_async_copy(cht.at[1, :, 0, :], chs, sem_lr.at[2])
    to_smem.start()
    to_smem.wait()
    slots += [slot_of(chs[0, 0]), slot_of(chs[1, 0])]
    envs[0].wait()
    set_right(0, slots[0])
    set_right(1, slots[1])
    l_copy.wait_recv()
    set_left(2, slots[2])
    set_left(3, slots[3])
    r_copy.wait_recv()
    set_right(2, slots[2])
    set_right(3, slots[3])
    ops_copy.wait_recv()
    for c in loads:
        c.wait()

    def prepare(k, w):
        b = w % 2
        for r in range(PH):
            col = slice(r * CH, (r + 1) * CH)
            for first in range(0, MS, 128):
                hi, lo = split(ext[k][slots[w], pl.ds(first * PH + r, 128, stride=PH), :])
                sx[b, first:first + 128, col] = hi
                sx[b, MS + first:MS + first + 128, col] = lo
                sx[b, 2 * MS + first:2 * MS + first + 128, col] = hi

    def stage1(k, w):
        b = w % 2
        zbuf[b] = jnp.dot(l3[w], sx[b], preferred_element_type=F32)
        step = 32
        for first in range(0, MS, step):
            parts = [zbuf[b, first:first + step, r * CH:(r + 1) * CH] for r in range(PH)]
            for p in range(PH):
                i = w * 16 + p * PH
                z = opv[i:i + 1, :] * parts[0]
                for r in range(1, PH):
                    z = z + opv[i + r:i + r + 1, :] * parts[r]
                hi, lo = split(z)
                rows = slice(p * MS + first, p * MS + first + step)
                base = w * 3 * CH
                x2[k % 2, rows, base:base + CH] = hi
                x2[k % 2, rows, base + CH:base + 2 * CH] = lo
                x2[k % 2, rows, base + 2 * CH:base + 3 * CH] = hi

    def stage2(k, p):
        part = jnp.dot(x2[k % 2, p * MS:(p + 1) * MS, :], r3[k], preferred_element_type=F32)
        part = part[:, 0:MS].reshape(4, 2, 2, OWN, MS)
        if k == 0:
            acc[p] = part
        else:
            acc[p] += part

    def via(u, i):
        src, dst = (acc.at[u, yop, i], vrx.at[u - 1, i]) if u else (acc.at[u, yop, xh, i], vrf.at[i])
        return remote(src, dst, sem_v.at[0, u, i], sem_v.at[1, u, i], (up, down)[i])

    def direct(u, i, b):
        row = (yup, ydn)[i]
        src, dst = (acc.at[u, row, b], yrx.at[u - 1, i, b]) if u else (acc.at[u, row, xh, b], yrf.at[i, b])
        return remote(src, dst, sem_y.at[0, u, i, b], sem_y.at[1, u, i, b], (up, down)[i])

    def exchange():
        return remote(acc.at[0, :, 1 - xh], xrf, sem_xf.at[0], sem_xf.at[1], xpart)

    def across(u, i):
        c = (core, other)[i]
        return remote(
            ysb.at[u - 1, 0, c], xrx.at[u - 1, i], sem_x.at[0, u - 1, i], sem_x.at[1, u - 1, i], (xpart, xdiag)[i])

    def swap(u):
        src = ysb.at[u - 1, 1, other] if u else fin.at[other]
        return remote(src, prx.at[u], sem_p.at[0, u], sem_p.at[1, u], partner)

    def s1(u):
        via(u, 0).start()
        via(u, 1).start()
        direct(u, 0, 1).start()
        direct(u, 1, 0).start()

    def s0():
        exchange().wait_recv()
        for row in (yop, yup, ydn, y):
            acc[0, row, xh] += xrf[row]

    def s2(u):
        for i in range(2):
            via(u, i).wait_recv()
            row = (yup, ydn)[i]
            if u:
                acc[u, row, i] += vrx[u - 1, i]
            else:
                acc[u, row, xh, i] += vrf[i]
            direct(u, i, i).start()

    def s3(u):
        for i in range(2):
            for b in range(2):
                direct(u, i, b).wait_recv()
        if u:
            for q, b in ((0, 1 - xh), (1, xh)):
                ysb[u - 1, q] = acc[u, y, b] + yrx[u - 1, 0, b] + yrx[u - 1, 1, b]
                if q == 0:
                    across(u, 0).start()
                    across(u, 1).start()
        else:
            fin[...] = acc[u, y, xh] + yrf[0] + yrf[1]
        swap(u).start()

    def s4(u):
        swap(u).wait_recv()
        if u:
            across(u, 0).wait_recv()
            across(u, 1).wait_recv()
            totals = ysb[u - 1, 1, core] + xrx[u - 1, 0], prx[u] + xrx[u - 1, 1]
        else:
            totals = fin[core], prx[u]
        col = slice(u * UNIT, (u + 1) * UNIT)
        for t, total in zip((core, other), totals):
            img[t, :, col] = (total + energy[t] * stw[t, :, col]) * msk[t, :, col]

    last = NCH - 1
    for k in range(NCH):
        arrive(k)
        for w in range(NW):
            prepare(k, w)
            stage1(k, w)
            if k < last and w == 1:
                pass_on(k + 1, 0)
                pass_on(k + 1, 1)
        for p in range(PH):
            stage2(k, p)
            if k == last and p == 0:
                exchange().start()
            elif k == last and p < 3:
                s1(p)
    s2(1)
    s1(3)
    s2(2)
    s3(1)
    s2(3)
    s0()
    s1(0)
    s3(2)
    s4(1)
    s3(3)
    s2(0)
    s4(2)
    s3(0)
    s4(3)
    s4(0)

    def total_of(x):
        x = jnp.sum(x, axis=0)
        return jnp.sum(jnp.sum(x, axis=0, keepdims=True), axis=1, keepdims=True)

    s, g, q = stw[...], img[...], inv[...]
    w_sum, c_sum = total_of(s * s), total_of(s * g)
    shift = jnp.where(w_sum > 0.0, c_sum / jnp.where(w_sum > 0.0, w_sum, 1.0), 0.0)
    m, v = s - (g - shift * s) * q, s * q
    a_sum, b_sum, d_sum = total_of(m * m), total_of(m * v), total_of(v * v)

    number = term * 8 + sec
    sub8 = lax.broadcasted_iota(jnp.int32, (8, 128), 0)
    lane8 = lax.broadcasted_iota(jnp.int32, (8, 128), 1)
    table = jnp.zeros((8, 128), F32)
    for i, v in enumerate((c_sum, w_sum, a_sum, b_sum, d_sum, shift)):
        table = jnp.where(sub8 == i, v, table)
    table = jnp.where(lane8 == number, table, 0.0)
    gt[0] = table

    def to_a(i):
        return remote(gt.at[0], ga.at[me_a], sem_ga.at[0, i], sem_ga.at[1, me_a], peer_a(i))

    def from_a(i):
        return remote(gt.at[0], ga.at[i], sem_ga.at[0, i], sem_ga.at[1, i], peer_a(i))

    def to_b(i):
        return remote(gt.at[1], gb.at[me_b], sem_gb.at[0, i], sem_gb.at[1, me_b], peer_b(i))

    def from_b(i):
        return remote(gt.at[1], gb.at[i], sem_gb.at[0, i], sem_gb.at[1, i], peer_b(i))

    for o in range(1, 8):
        to_a(lax.rem(me_a + o, 8)).start()
    for o in range(1, 8):
        i = lax.rem(me_a + o, 8)
        from_a(i).wait_recv()
        table = table + ga[i]
    gt[1] = table
    for o in range(1, 16):
        to_b(lax.rem(me_b + o, 16)).start()
    for o in range(1, 16):
        i = lax.rem(me_b + o, 16)
        from_b(i).wait_recv()
        table = table + gb[i]

    def row_sum(x):
        return jnp.sum(x, axis=1, keepdims=True)

    e_all = row_sum(table[0:1]) / row_sum(table[1:2])
    de = e_all - table[5:6]
    square = row_sum(table[2:3] + (2.0 * table[3:4] + de * table[4:5]) * de)
    scale = lax.rsqrt(square / (16.0 * MS * WIDE) + EPSILON)
    for t in range(2):
        for p in range(PH):
            col = slice(p * MS, (p + 1) * MS)
            s = stw[t, :, col]
            out[t, :, p, :] = (s - (img[t, :, col] - e_all * s) * inv[t, :, col]) * scale
    eng[0] = jnp.sum(e_all)

    for c in (size_copy, charge_copy, ops_copy, r_copy, l_copy):
        c.wait_send()
    for k in range(NCH):
        for i in range(2):
            piece(k, i).wait_send()
        if STRAIGHT[k]:
            straight(k).wait_send()
        for i in range(2):
            relay(k, i).wait_send()
    for u in range(NU):
        for i in range(2):
            via(u, i).wait_send()
            for b in range(2):
                direct(u, i, b).wait_send()
        if u:
            across(u, 0).wait_send()
            across(u, 1).wait_send()
        swap(u).wait_send()
    exchange().wait_send()
    for o in range(1, 8):
        to_a(lax.rem(me_a + o, 8)).wait_send()
    for o in range(1, 16):
        to_b(lax.rem(me_b + o, 16)).wait_send()


def body(psi, precond, left, right, ops, charge, sizes, energy):
    vm = pl.BlockSpec(memory_space=pltpu.VMEM)
    sm = pl.BlockSpec(memory_space=pltpu.SMEM)
    anyw = pl.BlockSpec(memory_space=pl.ANY)
    dma = pltpu.SemaphoreType.DMA
    return pl.pallas_call(
        kernel,
        out_shape=(
            jax.ShapeDtypeStruct((2, OWN, PH, MS), F32),
            jax.ShapeDtypeStruct((1,), F32),
        ),
        in_specs=[anyw, anyw, anyw, anyw, sm, sm, sm, sm],
        out_specs=(vm, sm),
        scratch_shapes=[
            pltpu.VMEM((3, MS * PH, CH), F32),
            pltpu.VMEM((3, MS * PH, CH), F32),
            pltpu.VMEM((3, MS * PH, CH), F32),
            pltpu.VMEM((3, 8, 128), jnp.int32),
            pltpu.VMEM((2, 8, 128), jnp.int32),
            pltpu.VMEM((64, 128), F32),
            pltpu.VMEM((2, 2, 8, 128), jnp.int32),
            pltpu.SMEM((2, 128), jnp.int32),
            pltpu.VMEM((NW, MS, MS), F32),
            pltpu.VMEM((NW, MS, MS), F32),
            pltpu.VMEM((NW, MS, 3 * MS), BF16),
            pltpu.VMEM((NCH, NW * 3 * CH, WPAD), BF16),
            pltpu.VMEM((2, 3 * MS, PH * CH), BF16),
            pltpu.VMEM((2, MS, PH * CH), F32),
            pltpu.VMEM((2, PH * MS, NW * 3 * CH), BF16),
            pltpu.VMEM((PH, 4, 2, 2, OWN, MS), F32),
            pltpu.VMEM((NU - 1, 2, 2, OWN, UNIT), F32),
            pltpu.VMEM((NU - 1, 2, 2, 2, OWN, UNIT), F32),
            pltpu.VMEM((NU - 1, 2, 2, OWN, UNIT), F32),
            pltpu.VMEM((NU - 1, 2, OWN, UNIT), F32),
            pltpu.VMEM((2, OWN, UNIT), F32),
            pltpu.VMEM((2, 2, OWN, UNIT), F32),
            pltpu.VMEM((4, 2, OWN, UNIT), F32),
            pltpu.VMEM((2, OWN, UNIT), F32),
            pltpu.VMEM((NU, OWN, UNIT), F32),
            pltpu.VMEM((2, OWN, PH, MS), F32),
            pltpu.VMEM((2, OWN, PH, MS), BF16),
            pltpu.VMEM((2, OWN, WIDE), F32),
            pltpu.VMEM((2, OWN, WIDE), F32),
            pltpu.VMEM((2, OWN, WIDE), F32),
            pltpu.VMEM((2, OWN, WIDE), F32),
            pltpu.VMEM((8, 8, 128), F32),
            pltpu.VMEM((16, 8, 128), F32),
            pltpu.VMEM((2, 8, 128), F32),
            dma((NCH, 2)),
            dma((2,)),
            dma((3,)),
            dma((2, 2)),
            dma((2, NCH, 2)),
            dma((2, NCH)),
            dma((2, NCH, 2)),
            dma((2,)),
            dma((2, 2)),
            dma((2, NU, 2)),
            dma((2, NU, 2, 2)),
            dma((2, NU - 1, 2)),
            dma((2,)),
            dma((2, NU)),
            dma((2, 8)),
            dma((2, 16)),
        ],
        compiler_params=pltpu.CompilerParams(
            collective_id=0, has_side_effects=True, vmem_limit_bytes=60 * 1024 * 1024
        ),
        name="update",
    )(psi, precond, left, right, ops, charge, sizes, energy)


def solution(mesh):
    in_specs = (
        P("sector", None, None, None),
        P("sector", None, None, None),
        P("term", "sector", None, None),
        P("term", "sector", None, None),
        P("term", None, None),
        P("term"),
        P("sector"),
        P("sector"),
    )
    out_specs = (P("sector", "term", None, None), P())
    return jax.shard_map(body, mesh=mesh, in_specs=in_specs, out_specs=out_specs, check_vma=False)
```

```python
import jax
import jax.numpy as jnp
from jax import lax
from jax.experimental import pallas as pl
from jax.experimental.pallas import tpu as pltpu
from jax.sharding import PartitionSpec as P

EPSILON = 1e-06
F32 = jnp.float32
BF16 = jnp.bfloat16
MS = 384
PH = 4
WPAD = 512
CH = 128
NCH = MS // CH
NW = 4
STRAIGHT = (192, 192, 192)
PIECE = (48, 48, 48)
OWN = MS // 16
WIDE = PH * MS
UNIT = MS
NU = WIDE // UNIT


def split(x):
    hi = x.astype(BF16)
    return hi, (x - hi.astype(F32)).astype(BF16)


def kernel(
    psi, precond, lenv, renv, ops, charge, sizes, energy,
    out, eng,
    ext0, ext1, ext2, extsz, szt, opv, cht, chs, lbuf, rbuf, l3, r3, sx, zbuf, x2, acc,
    vrx, yrx, ysb, xrx, vrf, yrf, xrf, fin, prx, stb, pcb, stw, inv, msk, img, ga, gb, gt,
    sem_in, sem_own, sem_lr, sem_er, sem_zq, sem_zd, sem_r, sem_sz, sem_cs, sem_v, sem_y, sem_x, sem_xf, sem_p, sem_ga, sem_gb,
):
    ext = (ext0, ext1, ext2)
    term = lax.axis_index("term")
    sec = lax.axis_index("sector")
    y = lax.div(term, 4)
    xh = lax.rem(lax.div(term, 2), 2)
    core = lax.rem(term, 2)
    other = 1 - core

    def dev(yy, hh, cc, ss=None):
        return {"term": yy * 4 + hh * 2 + cc, "sector": sec if ss is None else ss}

    partner = dev(y, xh, other)
    yup, ydn, yop = lax.rem(y + 1, 4), lax.rem(y + 3, 4), lax.rem(y + 2, 4)
    up, down = dev(yup, xh, core), dev(ydn, xh, core)
    xpart, xdiag = dev(y, 1 - xh, core), dev(y, 1 - xh, other)
    ahead = dev(y, xh, core, lax.rem(sec + 1 + 6 * core, 8))
    edge = sec == 7 * core

    me_a = y * 2 + core
    me_b = xh * 8 + sec

    def peer_a(i):
        return dev(lax.div(i, 2), xh, lax.rem(i, 2))

    def peer_b(i):
        return dev(y, lax.div(i, 8), core, lax.rem(i, 8))

    def rows_of(ref, first, n):
        return ref.at[pl.ds(pl.multiple_of(first * PH, 8), n * PH), :].reshape(n, PH, 128)

    own = [
        pltpu.make_async_copy(psi.at[:, pl.ds(term * OWN, OWN)], stb, sem_own.at[0]),
        pltpu.make_async_copy(precond.at[:, pl.ds(term * OWN, OWN)], pcb, sem_own.at[1]),
    ]
    envs = [
        pltpu.make_async_copy(renv.at[:, core], rbuf.at[pl.ds(0, 2)], sem_lr.at[0]),
        pltpu.make_async_copy(lenv.at[:, core], lbuf.at[pl.ds(0, 2)], sem_lr.at[1]),
    ]
    loads = []
    for k in range(NCH):
        for s in range(2):
            loads.append(pltpu.make_async_copy(
                psi.at[s, :, :, pl.ds(k * CH, CH)], rows_of(ext[k].at[1 + s], 0, MS), sem_in.at[k, s]))

    barrier = pltpu.get_barrier_semaphore()
    for o in range(1, 16):
        pl.semaphore_signal(barrier, inc=1, device_id=peer_b(lax.rem(me_b + o, 16)), device_id_type=pl.DeviceIdType.MESH)
    for o in range(1, 8):
        pl.semaphore_signal(barrier, inc=1, device_id=peer_a(lax.rem(me_a + o, 8)), device_id_type=pl.DeviceIdType.MESH)
    pl.semaphore_signal(barrier, inc=1, device_id=xdiag, device_id_type=pl.DeviceIdType.MESH)
    for c in own + envs + loads:
        c.start()

    for s in range(2):
        szt[s] = jnp.full((8, 128), sizes[s], jnp.int32)
        extsz[1 + s] = jnp.full((8, 128), sizes[s], jnp.int32)
    for w in range(2):
        cht[0, w] = jnp.full((8, 128), charge[w], jnp.int32)
        for p in range(PH):
            for r in range(PH):
                i = w * 16 + p * PH + r
                opv[i:i + 1, :] = jnp.full((1, 128), ops[w, p, r], F32)

    row_w = lax.broadcasted_iota(jnp.int32, (OWN, MS), 0) + term * OWN
    lane_w = lax.broadcasted_iota(jnp.int32, (OWN, MS), 1)
    for c in own:
        c.wait()
    for t in range(2):
        size = sizes[t]
        valid = (row_w < size) & (lane_w < size)
        mask = jnp.where(valid, 1.0, 0.0)
        for p in range(PH):
            msk[t, :, p * MS:(p + 1) * MS] = mask
            stw[t, :, p * MS:(p + 1) * MS] = jnp.where(valid, stb[t, :, p, :], 0.0)
            inv[t, :, p * MS:(p + 1) * MS] = 1.0 / pcb[t, :, p, :].astype(F32)

    def total_of(x):
        x = jnp.sum(x, axis=0)
        return jnp.sum(jnp.sum(x, axis=0, keepdims=True), axis=1, keepdims=True)

    w_sum = total_of(stw[...] * stw[...])
    d_sum = total_of((stw[...] * inv[...]) * (stw[...] * inv[...]))

    pl.semaphore_wait(barrier, 23)

    def remote(src, dst, s, r, where):
        return pltpu.make_async_remote_copy(
            src_ref=src, dst_ref=dst, send_sem=s, recv_sem=r, device_id=where, device_id_type=pl.DeviceIdType.MESH)

    def halo(k, first, n, sem, *i):
        return remote(
            psi.at[other, pl.ds(first, n), :, pl.ds(k * CH, CH)],
            rows_of(ext[k].at[0], first, n), sem.at[(0, k) + i], sem.at[(1, k) + i], ahead)

    def start_of(k, i):
        return STRAIGHT[k] + (lax.rem(y, 2) * 2 + i) * PIECE[k]

    def piece(k, i):
        return halo(k, start_of(k, i), PIECE[k], sem_zq, i)

    def straight(k):
        return halo(k, 0, STRAIGHT[k], sem_zd)

    def relay(k, i):
        ref = ext[k].at[0, pl.ds(pl.multiple_of(start_of(k, i) * PH, 8), PIECE[k] * PH), :]
        return remote(ref, ref, sem_r.at[0, k, i], sem_r.at[1, k, i], (up, down)[i])

    size_copy = remote(szt.at[other], extsz.at[0], sem_sz.at[0], sem_sz.at[1], ahead)
    charge_copy = remote(cht.at[0], cht.at[1], sem_cs.at[0, 0], sem_cs.at[1, 0], partner)
    ops_copy = remote(opv.at[pl.ds(0, 32)], opv.at[pl.ds(32, 32)], sem_cs.at[0, 1], sem_cs.at[1, 1], partner)
    r_copy = remote(renv.at[:, other], rbuf.at[pl.ds(2, 2)], sem_er.at[0, 0], sem_er.at[1, 0], partner)
    l_copy = remote(lenv.at[:, other], lbuf.at[pl.ds(2, 2)], sem_er.at[0, 1], sem_er.at[1, 1], partner)

    size_copy.start()
    charge_copy.start()
    ops_copy.start()
    for k in range(NCH):
        for i in range(2):
            piece(k, i).start()
        if STRAIGHT[k]:
            straight(k).start()
        if k == 0:
            l_copy.start()
            r_copy.start()
    r3[:, :, MS:WPAD] = jnp.zeros((NCH, NW * 3 * CH, WPAD - MS), BF16)

    size_copy.wait_recv()
    extsz[0] = jnp.where(edge, 0, extsz[0])
    row_m = lax.broadcasted_iota(jnp.int32, (MS, MS), 0)
    col_m = lax.broadcasted_iota(jnp.int32, (MS, MS), 1)

    def slot_of(c):
        rel = core - c
        return jnp.where((rel < 0) | (rel > 1), 0, rel + 1)

    def set_right(w, slot):
        size = jnp.concatenate([extsz[slot][0:1, :]] * NCH, axis=1)
        hi, lo = split(jnp.where(row_m < size, rbuf[w], 0.0))
        for k in range(NCH):
            cut = slice(k * CH, (k + 1) * CH)
            base = w * 3 * CH
            r3[k, base:base + CH, 0:MS] = hi[cut]
            r3[k, base + CH:base + 2 * CH, 0:MS] = hi[cut]
            r3[k, base + 2 * CH:base + 3 * CH, 0:MS] = lo[cut]

    def set_left(w, slot):
        size = jnp.concatenate([extsz[slot][0:1, :]] * NCH, axis=1)
        hi, lo = split(jnp.where(col_m < size, lbuf[w], 0.0))
        l3[w, :, 0:MS] = hi
        l3[w, :, MS:2 * MS] = hi
        l3[w, :, 2 * MS:3 * MS] = lo

    slots = [slot_of(charge[0]), slot_of(charge[1])]
    envs[1].wait()
    set_left(0, slots[0])

    def pass_on(k, i):
        piece(k, i).wait_recv()
        relay(k, i).start()

    def arrive(k):
        if STRAIGHT[k]:
            straight(k).wait_recv()
        for i in range(2):
            relay(k, i).wait_recv()

    pass_on(0, 0)
    set_left(1, slots[1])
    pass_on(0, 1)
    charge_copy.wait_recv()
    to_smem = pltpu.make_async_copy(cht.at[1, :, 0, :], chs, sem_lr.at[2])
    to_smem.start()
    to_smem.wait()
    slots += [slot_of(chs[0, 0]), slot_of(chs[1, 0])]
    envs[0].wait()
    set_right(0, slots[0])
    set_right(1, slots[1])
    l_copy.wait_recv()
    set_left(2, slots[2])
    set_left(3, slots[3])
    r_copy.wait_recv()
    set_right(2, slots[2])
    set_right(3, slots[3])
    ops_copy.wait_recv()
    for c in loads:
        c.wait()

    def prepare(k, w):
        b = w % 2
        for r in range(PH):
            col = slice(r * CH, (r + 1) * CH)
            for first in range(0, MS, 128):
                hi, lo = split(ext[k][slots[w], pl.ds(first * PH + r, 128, stride=PH), :])
                sx[b, first:first + 128, col] = hi
                sx[b, MS + first:MS + first + 128, col] = lo
                sx[b, 2 * MS + first:2 * MS + first + 128, col] = hi

    def stage1(k, w):
        b = w % 2
        zbuf[b] = jnp.dot(l3[w], sx[b], preferred_element_type=F32)
        step = 16
        for first in range(0, MS, step):
            parts = [zbuf[b, first:first + step, r * CH:(r + 1) * CH] for r in range(PH)]
            for p in range(PH):
                i = w * 16 + p * PH
                z = opv[i:i + 1, :] * parts[0]
                for r in range(1, PH):
                    z = z + opv[i + r:i + r + 1, :] * parts[r]
                hi, lo = split(z)
                rows = slice(p * MS + first, p * MS + first + step)
                base = w * 3 * CH
                x2[k % 2, rows, base:base + CH] = hi
                x2[k % 2, rows, base + CH:base + 2 * CH] = lo
                x2[k % 2, rows, base + 2 * CH:base + 3 * CH] = hi

    def stage2(k, p):
        part = jnp.dot(x2[k % 2, p * MS:(p + 1) * MS, :], r3[k], preferred_element_type=F32)
        part = part[:, 0:MS].reshape(4, 2, 2, OWN, MS)
        if k == 0:
            acc[p] = part
        else:
            acc[p] += part

    def via(u, i):
        src, dst = (acc.at[u, yop, i], vrx.at[u - 1, i]) if u else (acc.at[u, yop, xh, i], vrf.at[i])
        return remote(src, dst, sem_v.at[0, u, i], sem_v.at[1, u, i], (up, down)[i])

    def direct(u, i, b):
        row = (yup, ydn)[i]
        src, dst = (acc.at[u, row, b], yrx.at[u - 1, i, b]) if u else (acc.at[u, row, xh, b], yrf.at[i, b])
        return remote(src, dst, sem_y.at[0, u, i, b], sem_y.at[1, u, i, b], (up, down)[i])

    def exchange():
        return remote(acc.at[0, :, 1 - xh], xrf, sem_xf.at[0], sem_xf.at[1], xpart)

    def across(u, i):
        c = (core, other)[i]
        return remote(
            ysb.at[u - 1, 0, c], xrx.at[u - 1, i], sem_x.at[0, u - 1, i], sem_x.at[1, u - 1, i], (xpart, xdiag)[i])

    def swap(u):
        src = ysb.at[u - 1, 1, other] if u else fin.at[other]
        return remote(src, prx.at[u], sem_p.at[0, u], sem_p.at[1, u], partner)

    def s1(u):
        via(u, 0).start()
        via(u, 1).start()
        direct(u, 0, 1).start()
        direct(u, 1, 0).start()

    def s0():
        exchange().wait_recv()
        for row in (yop, yup, ydn, y):
            acc[0, row, xh] += xrf[row]

    def s2(u):
        for i in range(2):
            via(u, i).wait_recv()
            row = (yup, ydn)[i]
            if u:
                acc[u, row, i] += vrx[u - 1, i]
            else:
                acc[u, row, xh, i] += vrf[i]
            direct(u, i, i).start()

    def s3(u):
        for i in range(2):
            for b in range(2):
                direct(u, i, b).wait_recv()
        if u:
            for q, b in ((0, 1 - xh), (1, xh)):
                ysb[u - 1, q] = acc[u, y, b] + yrx[u - 1, 0, b] + yrx[u - 1, 1, b]
                if q == 0:
                    across(u, 0).start()
                    across(u, 1).start()
        else:
            fin[...] = acc[u, y, xh] + yrf[0] + yrf[1]
        swap(u).start()

    def s4(u):
        swap(u).wait_recv()
        if u:
            across(u, 0).wait_recv()
            across(u, 1).wait_recv()
            totals = ysb[u - 1, 1, core] + xrx[u - 1, 0], prx[u] + xrx[u - 1, 1]
        else:
            totals = fin[core], prx[u]
        col = slice(u * UNIT, (u + 1) * UNIT)
        for t, total in zip((core, other), totals):
            img[t, :, col] = (total + energy[t] * stw[t, :, col]) * msk[t, :, col]

    last = NCH - 1
    for k in range(NCH):
        arrive(k)
        for w in range(NW):
            prepare(k, w)
            stage1(k, w)
            if k < last and w == 1:
                pass_on(k + 1, 0)
                pass_on(k + 1, 1)
        for p in (1, 0, 2, 3):
            stage2(k, p)
            if k == last and p == 0:
                exchange().start()
            elif k == last and p < 3:
                s1(p)
    s2(1)
    s1(3)
    s2(2)
    s3(1)
    s2(3)
    s0()
    s1(0)
    s3(2)
    s4(1)
    s3(3)
    s2(0)
    s4(2)
    s3(0)
    s4(3)
    s4(0)

    s, g, q = stw[...], img[...], inv[...]
    c_sum = total_of(s * g)
    shift = jnp.where(w_sum > 0.0, c_sum / jnp.where(w_sum > 0.0, w_sum, 1.0), 0.0)
    v = s * q
    m = s - (g - shift * s) * q
    a_sum, b_sum = total_of(m * m), total_of(m * v)

    number = term * 8 + sec
    sub8 = lax.broadcasted_iota(jnp.int32, (8, 128), 0)
    lane8 = lax.broadcasted_iota(jnp.int32, (8, 128), 1)
    table = jnp.zeros((8, 128), F32)
    for i, v in enumerate((c_sum, w_sum, a_sum, b_sum, d_sum, shift)):
        table = jnp.where(sub8 == i, v, table)
    table = jnp.where(lane8 == number, table, 0.0)
    gt[0] = table

    def to_a(i):
        return remote(gt.at[0], ga.at[me_a], sem_ga.at[0, i], sem_ga.at[1, me_a], peer_a(i))

    def from_a(i):
        return remote(gt.at[0], ga.at[i], sem_ga.at[0, i], sem_ga.at[1, i], peer_a(i))

    def to_b(i):
        return remote(gt.at[1], gb.at[me_b], sem_gb.at[0, i], sem_gb.at[1, me_b], peer_b(i))

    def from_b(i):
        return remote(gt.at[1], gb.at[i], sem_gb.at[0, i], sem_gb.at[1, i], peer_b(i))

    for o in range(1, 8):
        to_a(lax.rem(me_a + o, 8)).start()
    for o in range(1, 8):
        i = lax.rem(me_a + o, 8)
        from_a(i).wait_recv()
        table = table + ga[i]
    gt[1] = table
    for o in range(1, 16):
        to_b(lax.rem(me_b + o, 16)).start()
    for o in range(1, 16):
        i = lax.rem(me_b + o, 16)
        from_b(i).wait_recv()
        table = table + gb[i]

    def row_sum(x):
        return jnp.sum(x, axis=1, keepdims=True)

    e_all = row_sum(table[0:1]) / row_sum(table[1:2])
    de = e_all - table[5:6]
    square = row_sum(table[2:3] + (2.0 * table[3:4] + de * table[4:5]) * de)
    scale = lax.rsqrt(square / (16.0 * MS * WIDE) + EPSILON)
    for t in range(2):
        for p in range(PH):
            col = slice(p * MS, (p + 1) * MS)
            s = stw[t, :, col]
            out[t, :, p, :] = (s - (img[t, :, col] - e_all * s) * inv[t, :, col]) * scale
    eng[0] = jnp.sum(e_all)

    for c in (size_copy, charge_copy, ops_copy, r_copy, l_copy):
        c.wait_send()
    for k in range(NCH):
        for i in range(2):
            piece(k, i).wait_send()
        if STRAIGHT[k]:
            straight(k).wait_send()
        for i in range(2):
            relay(k, i).wait_send()
    for u in range(NU):
        for i in range(2):
            via(u, i).wait_send()
            for b in range(2):
                direct(u, i, b).wait_send()
        if u:
            across(u, 0).wait_send()
            across(u, 1).wait_send()
        swap(u).wait_send()
    exchange().wait_send()
    for o in range(1, 8):
        to_a(lax.rem(me_a + o, 8)).wait_send()
    for o in range(1, 16):
        to_b(lax.rem(me_b + o, 16)).wait_send()


def body(psi, precond, left, right, ops, charge, sizes, energy):
    vm = pl.BlockSpec(memory_space=pltpu.VMEM)
    sm = pl.BlockSpec(memory_space=pltpu.SMEM)
    anyw = pl.BlockSpec(memory_space=pl.ANY)
    dma = pltpu.SemaphoreType.DMA
    return pl.pallas_call(
        kernel,
        out_shape=(
            jax.ShapeDtypeStruct((2, OWN, PH, MS), F32),
            jax.ShapeDtypeStruct((1,), F32),
        ),
        in_specs=[anyw, anyw, anyw, anyw, sm, sm, sm, sm],
        out_specs=(vm, sm),
        scratch_shapes=[
            pltpu.VMEM((3, MS * PH, CH), F32),
            pltpu.VMEM((3, MS * PH, CH), F32),
            pltpu.VMEM((3, MS * PH, CH), F32),
            pltpu.VMEM((3, 8, 128), jnp.int32),
            pltpu.VMEM((2, 8, 128), jnp.int32),
            pltpu.VMEM((64, 128), F32),
            pltpu.VMEM((2, 2, 8, 128), jnp.int32),
            pltpu.SMEM((2, 128), jnp.int32),
            pltpu.VMEM((NW, MS, MS), F32),
            pltpu.VMEM((NW, MS, MS), F32),
            pltpu.VMEM((NW, MS, 3 * MS), BF16),
            pltpu.VMEM((NCH, NW * 3 * CH, WPAD), BF16),
            pltpu.VMEM((2, 3 * MS, PH * CH), BF16),
            pltpu.VMEM((2, MS, PH * CH), F32),
            pltpu.VMEM((2, PH * MS, NW * 3 * CH), BF16),
            pltpu.VMEM((PH, 4, 2, 2, OWN, MS), F32),
            pltpu.VMEM((NU - 1, 2, 2, OWN, UNIT), F32),
            pltpu.VMEM((NU - 1, 2, 2, 2, OWN, UNIT), F32),
            pltpu.VMEM((NU - 1, 2, 2, OWN, UNIT), F32),
            pltpu.VMEM((NU - 1, 2, OWN, UNIT), F32),
            pltpu.VMEM((2, OWN, UNIT), F32),
            pltpu.VMEM((2, 2, OWN, UNIT), F32),
            pltpu.VMEM((4, 2, OWN, UNIT), F32),
            pltpu.VMEM((2, OWN, UNIT), F32),
            pltpu.VMEM((NU, OWN, UNIT), F32),
            pltpu.VMEM((2, OWN, PH, MS), F32),
            pltpu.VMEM((2, OWN, PH, MS), BF16),
            pltpu.VMEM((2, OWN, WIDE), F32),
            pltpu.VMEM((2, OWN, WIDE), F32),
            pltpu.VMEM((2, OWN, WIDE), F32),
            pltpu.VMEM((2, OWN, WIDE), F32),
            pltpu.VMEM((8, 8, 128), F32),
            pltpu.VMEM((16, 8, 128), F32),
            pltpu.VMEM((2, 8, 128), F32),
            dma((NCH, 2)),
            dma((2,)),
            dma((3,)),
            dma((2, 2)),
            dma((2, NCH, 2)),
            dma((2, NCH)),
            dma((2, NCH, 2)),
            dma((2,)),
            dma((2, 2)),
            dma((2, NU, 2)),
            dma((2, NU, 2, 2)),
            dma((2, NU - 1, 2)),
            dma((2,)),
            dma((2, NU)),
            dma((2, 8)),
            dma((2, 16)),
        ],
        compiler_params=pltpu.CompilerParams(
            collective_id=0, has_side_effects=True, vmem_limit_bytes=60 * 1024 * 1024
        ),
        name="update",
    )(psi, precond, left, right, ops, charge, sizes, energy)


def solution(mesh):
    in_specs = (
        P("sector", None, None, None),
        P("sector", None, None, None),
        P("term", "sector", None, None),
        P("term", "sector", None, None),
        P("term", None, None),
        P("term"),
        P("sector"),
        P("sector"),
    )
    out_specs = (P("sector", "term", None, None), P())
    return jax.shard_map(body, mesh=mesh, in_specs=in_specs, out_specs=out_specs, check_vma=False)
```
